32 devices in a mesh: atom: 8 (over z, core), kvec: 4 (over y, x).
Axes of the slice: x: 2, y: 2, z: 4, core: 2. Of those that a mesh axis runs over, the one named last changes fastest.
Arguments:
- features: float32 [12288, 256], P(('atom', 'kvec')), may hold values from -6 to 6
- fractions: int32 [3, 12288], P(None, 'atom'), may hold values from 0 to 1023
- wave_index: int32 [3, 2048], P(None, 'kvec'), may hold values from -12 to 12
- brick_count: int32 [8], replicated, may hold values from 1 to 1536, 6144 in all
- value_weight: float32 [256, 256], replicated, may hold values from -0.375 to 0.375
- k_filter: float32 [2, 2048, 256], P(None, 'kvec'), may hold values from -6 to 6
- mix_weight: float32 [2, 256, 256], replicated, may hold values from -0.25 to 0.25
- out_weight: float32 [256, 256], replicated, may hold values from -0.375 to 0.375
- norm_gain: float32 [256], replicated, may hold values from 0.5 to 1.5
- up_weight: float32 [256, 512], replicated, may hold values from -0.375 to 0.375
- down_weight: float32 [512, 256], replicated, may hold values from -0.25 to 0.25
Outputs:
- updated: float32 [12288, 256], P(('atom', 'kvec'))
The draws below stay inside these ranges and needn't reach their ends.
Inputs may be any that keep to these rules, and one draw needn't show every extreme that they name: Brick b holds its atoms in its first brick_count[b] slots; the counts sum to 6144 and the largest equals 1536.
All inputs are finite; a program needn't handle non-finite values.
Results may differ from the reference program's by a relative error of at most 0.0003.
Values sent between devices are 32-bit elements; how exact they have to be, the bound alone decides.
A program may use at most 64 MiB of HBM per device.

```python
import math
import jax
import jax.numpy as jnp
import numpy as np
from jax import lax

W = 256
HID = 512
CAP = 1536
K = 2048
ATOMS_PAD = 12288
TOTAL = 6144
N_ATOM = 8


def touch_ends(result, key, low, high):
    spot = [jax.random.randint(jax.random.fold_in(key, axis), (), 0, length) for axis, length in enumerate(result.shape)]
    widest = result.shape.index(max(result.shape))
    next_to = spot[:widest] + [(spot[widest] + 1) % result.shape[widest]] + spot[widest + 1:]
    return result.at[tuple(spot)].set(low).at[tuple(next_to)].set(high)


def block_levels(stream_key, shape, cuts, low, largest):
    level, own = 1.0, jax.random.fold_in(stream_key, 6)
    for dim, parts in cuts:
        draws = jnp.exp(jax.random.uniform(jax.random.fold_in(own, dim), (parts,), jnp.float32, low / len(cuts), largest / len(cuts)))
        level = level * jnp.repeat(draws, shape[dim] // parts).reshape([-1 if axis == dim else 1 for axis in range(len(shape))])
    return level


def split_up(number_of, total, most, lean):
    portions = [(1 << 20) // math.isqrt(standing ** lean) + 1 for standing in range(2, number_of + 1)]
    rest, given = total - most - (number_of - 1), [1] * (number_of - 1)
    while rest > 0:
        movable = [i for i in range(number_of - 1) if given[i] < most]
        whole, budget = sum([portions[i] for i in movable]), rest
        for i in movable:
            addition = min(most - given[i], max(1, budget * portions[i] // whole), rest)
            given[i] = given[i] + addition
            rest = rest - addition
    return np.array([most] + given)


def ragged_sizes(rng, amount, total, bound, skew):
    if amount == 2:
        one = jax.random.randint(rng, (), max(1, total - bound), min(bound, total - 1) + 1)
        return jnp.stack([one, total - one])
    tallies = jnp.asarray(split_up(amount, total, bound, skew), jnp.int32)
    pairs = (amount - 1) // 2
    source_of, taker = tallies[1:1 + 2 * pairs:2], tallies[2:2 + 2 * pairs:2]
    room = jnp.minimum(source_of - 1, bound - taker)
    shifted = jax.random.randint(jax.random.fold_in(rng, 1), (pairs,), 0, 1 << 20) % (room + 1)
    tallies = tallies.at[1:1 + 2 * pairs:2].set(source_of - shifted).at[2:2 + 2 * pairs:2].set(taker + shifted)
    return tallies[jax.random.permutation(jax.random.fold_in(rng, 2), amount)]


def centred(rng, shape, deviation, limit, shards=(), kind=jnp.bfloat16):
    level = block_levels(rng, shape, shards, -0.22, 0.18) if shards else 1.0
    result = jax.random.normal(rng, shape, jnp.float32) * deviation * level
    return jnp.minimum(jnp.maximum(result, -limit), limit).astype(kind)


def setup_inputs(seed: int = 0) -> dict:
    streams_of = jax.random.split(jax.random.key(seed), 12)
    return {
        "features": centred(streams_of[0], (ATOMS_PAD, W), 1.0, 6.0, ((0, 32),), jnp.float32),
        "fractions": touch_ends(jax.random.randint(streams_of[1], (3, ATOMS_PAD), 0, 1024), jax.random.fold_in(streams_of[1], 1), 0, 1023).astype(jnp.int32),
        "wave_index": touch_ends(jax.random.randint(streams_of[2], (3, K), -12, 13), jax.random.fold_in(streams_of[2], 1), -12, 12).astype(jnp.int32),
        "brick_count": ragged_sizes(streams_of[3], N_ATOM, TOTAL, CAP, 2).astype(jnp.int32),
        "value_weight": centred(streams_of[4], (W, W), W ** -0.5, 0.375, (), jnp.float32),
        "k_filter": centred(streams_of[5], (2, K, W), 1.0, 6.0, ((1, 4),), jnp.float32),
        "mix_weight": centred(streams_of[6], (2, W, W), (2 * W) ** -0.5, 0.25, (), jnp.float32),
        "out_weight": centred(streams_of[7], (W, W), W ** -0.5, 0.375, (), jnp.float32),
        "norm_gain": jnp.clip(1.0 + 0.1 * jax.random.normal(streams_of[8], (W,), jnp.float32), 0.5, 1.5),
        "up_weight": centred(streams_of[9], (W, HID), W ** -0.5, 0.375, (), jnp.float32),
        "down_weight": centred(streams_of[10], (HID, W), HID ** -0.5, 0.25, (), jnp.float32),
    }


phase_step = 2.0 * math.pi / 1024.0
exact = lax.Precision.HIGHEST

def phases(frac_rows, wave_index):
    phase_index = frac_rows[0][:, None] * wave_index[0][None, :]
    phase_index = phase_index + frac_rows[1][:, None] * wave_index[1][None, :]
    phase_index = phase_index + frac_rows[2][:, None] * wave_index[2][None, :]
    angles = jnp.mod(phase_index, 1024).astype(jnp.float32) * phase_step
    return (jnp.cos(angles), jnp.sin(angles))

def mixing(real_part, imag_part, filt_real, filt_imag, mix_weight, normalizer):
    mixed_real = real_part * filt_real - imag_part * filt_imag
    mixed_imag = real_part * filt_imag + imag_part * filt_real
    out_real = (jnp.dot(mixed_real, mix_weight[0], precision=exact) - jnp.dot(mixed_imag, mix_weight[1], precision=exact)) * normalizer
    out_imag = (jnp.dot(mixed_real, mix_weight[1], precision=exact) + jnp.dot(mixed_imag, mix_weight[0], precision=exact)) * normalizer
    return (out_real, out_imag)

def reference(features, fractions, wave_index, brick_count, value_weight, k_filter, mix_weight, out_weight, norm_gain, up_weight, down_weight):
    slots = jnp.arange(CAP, dtype=jnp.int32)
    live_mask = (slots[None, :] < brick_count[:, None]).astype(jnp.float32).reshape(N_ATOM * CAP)
    values = jnp.dot(features, value_weight, precision=exact) * live_mask[:, None]
    brick_values = values.reshape(N_ATOM, CAP, W)
    brick_fracs = jnp.transpose(fractions.reshape(3, N_ATOM, CAP), (1, 0, 2))

    def collect(partial_value, item):
        value_rows, frac_rows = item
        cosine, sine_part = phases(frac_rows, wave_index)
        real_part = partial_value[0] + jnp.dot(cosine.T, value_rows, precision=exact)
        imag_part = partial_value[1] - jnp.dot(sine_part.T, value_rows, precision=exact)
        return ((real_part, imag_part), None)
    empty_sums = jnp.zeros((K, W), jnp.float32)
    (real_sf, imag_sf), unused = lax.scan(collect, (empty_sums, empty_sums), (brick_values, brick_fracs))
    normalizer = 1.0 / math.sqrt(TOTAL * K)
    filt_real, filt_imag = mixing(real_sf, imag_sf, k_filter[0], k_filter[1], mix_weight, normalizer)

    def project_back(frac_rows):
        cosine, sine_part = phases(frac_rows, wave_index)
        return jnp.dot(cosine, filt_real, precision=exact) - jnp.dot(sine_part, filt_imag, precision=exact)
    messages = lax.map(project_back, brick_fracs).reshape(N_ATOM * CAP, W)
    residual = features + jnp.dot(messages, out_weight, precision=exact)
    normed = residual * lax.rsqrt(lax.optimization_barrier(jnp.mean(residual * residual, axis=1, keepdims=True)) + 1e-06) * norm_gain
    hidden = jax.nn.silu(jnp.dot(normed, up_weight, precision=exact))
    return (residual + jnp.dot(hidden, down_weight, precision=exact)) * live_mask[:, None]
```

```python
import functools
import math

import jax
import jax.numpy as jnp
from jax import lax
from jax.experimental import pallas as pl
from jax.experimental.pallas import tpu as pltpu
from jax.sharding import PartitionSpec as P

SIN_POLY = (3.141592640130707, -5.167710083507862, 2.550077523214134, -0.5982912856178576, 0.0776576603009221)
COS_POLY = (0.9999999997799045, -4.9348021370788056, 4.058709159555753, -1.3352120030448535, 0.23493731379172217, -0.024396324310603436)
MESH = pl.DeviceIdType.MESH
f32 = jnp.float32
bf16 = jnp.bfloat16


def horner(coefs, y):
    acc = jnp.full_like(y, coefs[-1])
    for c in coefs[-2::-1]:
        acc = acc * y + c
    return acc


def split(x):
    hi = x.astype(bf16)
    return hi, (x - hi.astype(f32)).astype(bf16)


def mm(a, b):
    return jnp.dot(a, b, preferred_element_type=f32)


def mm3(a, b):
    return mm(a[0], b[0]) + (mm(a[0], b[1]) + mm(a[1], b[0]))


def kernel(
    groups,
    bricks,
    normalizer,
    count_ref,
    feat_ref,
    frac_t_ref,
    frac_n_ref,
    wave_t_ref,
    wave_n_ref,
    gain_ref,
    kf_hbm,
    vw_hbm,
    mix_hbm,
    ow_hbm,
    up_hbm,
    down_hbm,
    out_ref,
    kf,
    vw,
    mix,
    ow,
    up,
    down,
    phase_t,
    phase_n,
    ct,
    cn,
    xbuf,
    sacc,
    pbuf,
    ssum,
    rbuf,
    tsl,
    tbuf,
    mbuf,
    gbuf,
    load_sem,
    x_send,
    x_recv,
    p_send,
    p_recv,
    r_send,
    r_recv,
    t_send,
    t_recv,
    q_send,
    q_recv,
    m_send,
    m_recv,
):
    rows, width = feat_ref.shape
    k_shard = kf.shape[1]
    half = k_shard // 2
    z_size = bricks // 2
    piece = half // z_size
    a = lax.axis_index("atom")
    g = lax.axis_index("kvec")
    z = lax.div(a, 2)
    c = lax.rem(a, 2)
    partner = 2 * z + 1 - c
    count = count_ref[0]

    def z_peer(d):
        return 2 * lax.rem(z + d, z_size) + c

    def z_from(d):
        return lax.rem(z + z_size - d, z_size)

    barrier = pltpu.get_barrier_semaphore()
    for d in range(1, groups):
        pl.semaphore_signal(
            barrier, inc=1, device_id={"kvec": lax.rem(g + d, groups)}, device_id_type=MESH
        )
    for d in range(1, z_size):
        pl.semaphore_signal(
            barrier, inc=1, device_id={"atom": z_peer(d)}, device_id_type=MESH
        )
    pl.semaphore_signal(barrier, inc=1, device_id={"atom": partner}, device_id_type=MESH)

    loads = []
    for i, (src, dst) in enumerate(
        ((kf_hbm, kf), (vw_hbm, vw), (mix_hbm, mix), (ow_hbm, ow), (up_hbm, up), (down_hbm, down))
    ):
        loads.append(pltpu.make_async_copy(src, dst, load_sem.at[i]))
        loads[-1].start()

    pl.semaphore_wait(barrier, groups - 1 + z_size)

    def x_copy(d):
        return pltpu.make_async_remote_copy(
            src_ref=feat_ref,
            dst_ref=xbuf.at[g],
            send_sem=x_send.at[d - 1],
            recv_sem=x_recv.at[d - 1],
            device_id={"kvec": lax.rem(g + d, groups)},
            device_id_type=MESH,
        )

    for d in range(1, groups):
        x_copy(d).start()

    def table(dst, j, phase, lead, step):
        def one(i, carry):
            at = pl.multiple_of(i * step, step)
            x = phase[pl.ds(at, step), :]
            r = x - jnp.floor(x + 0.5)
            y = r * r
            s = r * horner(SIN_POLY, y)
            co = horner(COS_POLY, y)
            s2 = s + s
            chi, clo = split(1.0 - s2 * s)
            shi, slo = split(s2 * co)
            dst[0, j, pl.ds(at, step), :] = chi
            dst[1, j, pl.ds(at, step), :] = clo
            dst[2, j, pl.ds(at, step), :] = shi
            dst[3, j, pl.ds(at, step), :] = slo
            return carry

        lax.fori_loop(0, lead // step, one, 0, unroll=2)

    def make_tables(j, carry):
        phase_t[...] = mm(wave_t_ref[...], frac_t_ref[j])
        table(ct, j, phase_t, k_shard, 32)
        phase_n[...] = mm(frac_n_ref[j], wave_n_ref[...])
        table(cn, j, phase_n, rows, 16)
        return carry

    lax.fori_loop(0, groups, make_tables, 0)

    def live(j):
        spot = lax.broadcasted_iota(jnp.int32, (rows, width), 0) + j * rows
        return spot < count

    def gather_term(x, j):
        v = split(jnp.where(live(j), x, 0.0))
        re = mm3((ct[0, j], ct[1, j]), v)
        im = mm3((ct[2, j], ct[3, j]), v)
        return (
            re.reshape(2, z_size, piece, width),
            im.reshape(2, z_size, piece, width),
        )

    re, im = gather_term(feat_ref[...], g)
    sacc[:, :, 0] = re
    sacc[:, :, 1] = im

    def take_block(d, carry):
        j = lax.rem(g + groups - d, groups)
        x_copy(d).wait_recv()
        re, im = gather_term(xbuf[j], j)
        sacc[:, :, 0] += re
        sacc[:, :, 1] += im
        return carry

    lax.fori_loop(1, groups, take_block, 0)

    pair = pltpu.make_async_remote_copy(
        src_ref=sacc.at[1 - c],
        dst_ref=pbuf,
        send_sem=p_send,
        recv_sem=p_recv,
        device_id={"atom": partner},
        device_id_type=MESH,
    )
    pair.start()
    pair.wait_recv()
    ssum[...] = sacc[c] + pbuf[...]

    def r_copy(d):
        return pltpu.make_async_remote_copy(
            src_ref=ssum.at[lax.rem(z + d, z_size)],
            dst_ref=rbuf.at[d - 1],
            send_sem=r_send.at[d - 1],
            recv_sem=r_recv.at[d - 1],
            device_id={"atom": z_peer(d)},
            device_id_type=MESH,
        )

    for d in range(1, z_size):
        r_copy(d).start()
    for load in loads:
        load.wait()
    vws = split(vw[...])
    mix_re = split(mix[0])
    mix_im = split(mix[1])
    total = ssum[z]
    for d in range(1, z_size):
        r_copy(d).wait_recv()
        total = total + rbuf[d - 1]
    sv = mm3(split(total.reshape(2 * piece, width)), vws)
    sre = sv[:piece]
    sim = -sv[piece:]
    at = pl.multiple_of(c * half + z * piece, piece)
    k_re = kf[0, pl.ds(at, piece), :]
    k_im = kf[1, pl.ds(at, piece), :]
    u_re = split(sre * k_re - sim * k_im)
    u_im = split(sre * k_im + sim * k_re)
    tsl[0] = (mm3(u_re, mix_re) - mm3(u_im, mix_im)) * normalizer
    tsl[1] = (mm3(u_re, mix_im) + mm3(u_im, mix_re)) * normalizer

    def t_copy(d):
        return pltpu.make_async_remote_copy(
            src_ref=tsl,
            dst_ref=tbuf.at[c, z],
            send_sem=t_send.at[d - 1],
            recv_sem=t_recv.at[d - 1],
            device_id={"atom": z_peer(d)},
            device_id_type=MESH,
        )

    def q_copy(d):
        return pltpu.make_async_remote_copy(
            src_ref=tsl if d == 0 else tbuf.at[c, z_from(d)],
            dst_ref=tbuf.at[c, z_from(d)],
            send_sem=q_send.at[d],
            recv_sem=q_recv.at[d],
            device_id={"atom": partner},
            device_id_type=MESH,
        )

    for d in range(1, z_size):
        t_copy(d).start()
    q_copy(0).start()
    tbuf[c, z] = tsl[...]
    for d in range(1, z_size):
        t_copy(d).wait_recv()
        q_copy(d).start()
    for d in range(z_size):
        q_copy(d).wait_recv()

    t_re = split(tbuf[:, :, 0].reshape(k_shard, width))
    t_im = split(tbuf[:, :, 1].reshape(k_shard, width))

    def message(j):
        return mm3((cn[0, j], cn[1, j]), t_re) - mm3((cn[2, j], cn[3, j]), t_im)

    def m_copy(d):
        return pltpu.make_async_remote_copy(
            src_ref=mbuf.at[d - 1],
            dst_ref=gbuf.at[d - 1],
            send_sem=m_send.at[d - 1],
            recv_sem=m_recv.at[d - 1],
            device_id={"kvec": lax.rem(g + d, groups)},
            device_id_type=MESH,
        )

    def give_block(d, carry):
        mbuf[d - 1] = message(lax.rem(g + d, groups))
        m_copy(d).start()
        return carry

    lax.fori_loop(1, groups, give_block, 0)
    own = message(g)
    for d in range(1, groups):
        m_copy(d).wait_recv()
        own = own + gbuf[d - 1]

    residual = feat_ref[...] + mm3(split(own), split(ow[...]))
    scale = lax.rsqrt(jnp.mean(residual * residual, axis=1, keepdims=True) + 1e-06)
    normed = residual * scale * gain_ref[...]
    raised = mm3(split(normed), split(up[...]))
    hidden = raised / (1.0 + jnp.exp(-raised))
    result = residual + mm3(split(hidden), split(down[...]))
    out_ref[...] = jnp.where(live(g), result, 0.0)

    for d in range(1, groups):
        x_copy(d).wait_send()
        m_copy(d).wait_send()
    pair.wait_send()
    for d in range(1, z_size):
        r_copy(d).wait_send()
        t_copy(d).wait_send()
    for d in range(z_size):
        q_copy(d).wait_send()


def shards(
    features,
    fractions,
    wave_index,
    brick_count,
    value_weight,
    k_filter,
    mix_weight,
    out_weight,
    norm_gain,
    up_weight,
    down_weight,
):
    rows, width = features.shape
    groups = lax.axis_size("kvec")
    bricks = lax.axis_size("atom")
    k_shard = wave_index.shape[1]
    hidden = up_weight.shape[1]
    capacity = rows * groups
    z_size = bricks // 2
    piece = k_shard // bricks
    normalizer = 1.0 / math.sqrt(bricks * capacity // 2 * (k_shard * groups))
    own_brick = lax.axis_index("atom")
    brick_ids = jnp.arange(bricks, dtype=jnp.int32)
    count = jnp.sum(jnp.where(brick_ids == own_brick, brick_count, 0)).reshape(1)

    frac = jnp.concatenate(
        [
            (fractions >> 5).astype(f32) * (1.0 / 32),
            (fractions & 31).astype(f32) * (1.0 / 1024),
            jnp.zeros((10, capacity), f32),
        ],
        axis=0,
    ).astype(bf16)
    frac_t = frac.reshape(16, groups, rows).transpose(1, 0, 2)
    frac_n = frac.reshape(16, groups, rows).transpose(1, 2, 0)
    wave = wave_index.astype(f32)
    wave_n = jnp.concatenate([wave, wave, jnp.zeros((10, k_shard), f32)], axis=0).astype(bf16)
    wave_t = wave_n.T

    vmem = pl.BlockSpec(memory_space=pltpu.VMEM)
    hbm = pl.BlockSpec(memory_space=pl.ANY)
    dma = pltpu.SemaphoreType.DMA
    return pl.pallas_call(
        functools.partial(kernel, groups, bricks, normalizer),
        out_shape=jax.ShapeDtypeStruct((rows, width), f32),
        in_specs=[pl.BlockSpec(memory_space=pltpu.SMEM)] + [vmem] * 6 + [hbm] * 6,
        out_specs=vmem,
        scratch_shapes=[
            pltpu.VMEM((2, k_shard, width), f32),
            pltpu.VMEM((width, width), f32),
            pltpu.VMEM((2, width, width), f32),
            pltpu.VMEM((width, width), f32),
            pltpu.VMEM((width, hidden), f32),
            pltpu.VMEM((hidden, width), f32),
            pltpu.VMEM((k_shard, rows), f32),
            pltpu.VMEM((rows, k_shard), f32),
            pltpu.VMEM((4, groups, k_shard, rows), bf16),
            pltpu.VMEM((4, groups, rows, k_shard), bf16),
            pltpu.VMEM((groups, rows, width), f32),
            pltpu.VMEM((2, z_size, 2, piece, width), f32),
            pltpu.VMEM((z_size, 2, piece, width), f32),
            pltpu.VMEM((z_size, 2, piece, width), f32),
            pltpu.VMEM((z_size - 1, 2, piece, width), f32),
            pltpu.VMEM((2, piece, width), f32),
            pltpu.VMEM((2, z_size, 2, piece, width), f32),
            pltpu.VMEM((groups - 1, rows, width), f32),
            pltpu.VMEM((groups - 1, rows, width), f32),
            dma((6,)),
            dma((groups - 1,)),
            dma((groups - 1,)),
            dma,
            dma,
            dma((z_size - 1,)),
            dma((z_size - 1,)),
            dma((z_size - 1,)),
            dma((z_size - 1,)),
            dma((z_size,)),
            dma((z_size,)),
            dma((groups - 1,)),
            dma((groups - 1,)),
        ],
        compiler_params=pltpu.CompilerParams(
            collective_id=0, has_side_effects=True, vmem_limit_bytes=56 * 1024 * 1024
        ),
    )(
        count,
        features,
        frac_t,
        frac_n,
        wave_t,
        wave_n,
        norm_gain.reshape(1, width),
        k_filter,
        value_weight,
        mix_weight,
        out_weight,
        up_weight,
        down_weight,
    )


def solution(mesh):
    return jax.shard_map(
        shards,
        mesh=mesh,
        in_specs=(
            P(("atom", "kvec"), None),
            P(None, "atom"),
            P(None, "kvec"),
            P(),
            P(),
            P(None, "kvec", None),
            P(),
            P(),
            P(),
            P(),
            P(),
        ),
        out_specs=P(("atom", "kvec"), None),
        check_vma=False,
    )
```

```python
import functools
import math

import jax
import jax.numpy as jnp
from jax import lax
from jax.experimental import pallas as pl
from jax.experimental.pallas import tpu as pltpu
from jax.sharding import PartitionSpec as P

SIN_POLY = (3.141592640130707, -5.167710083507862, 2.550077523214134, -0.5982912856178576, 0.0776576603009221)
COS_POLY = (0.9999999997799045, -4.9348021370788056, 4.058709159555753, -1.3352120030448535, 0.23493731379172217, -0.024396324310603436)
PARTS = 2
MESH = pl.DeviceIdType.MESH
f32 = jnp.float32
bf16 = jnp.bfloat16


def horner(coefs, y):
    acc = jnp.full_like(y, coefs[-1])
    for c in coefs[-2::-1]:
        acc = acc * y + c
    return acc


def split(x):
    hi = x.astype(bf16)
    return hi, (x - hi.astype(f32)).astype(bf16)


def mm(a, b):
    return jnp.dot(a, b, preferred_element_type=f32)


def mm3(a, b):
    return mm(a[0], b[0]) + (mm(a[0], b[1]) + mm(a[1], b[0]))


def kernel(
    groups,
    bricks,
    normalizer,
    count_ref,
    feat_ref,
    frac_ref,
    wave_ref,
    gain_ref,
    kf_hbm,
    vw_hbm,
    mix_hbm,
    ow_hbm,
    up_hbm,
    down_hbm,
    out_ref,
    kf,
    vw,
    mix,
    ow,
    up,
    down,
    frac,
    phase_t,
    phase_n,
    ct,
    cn,
    xbuf,
    sacc,
    pbuf,
    ssum,
    rbuf,
    tsl,
    tbuf,
    mbuf,
    gbuf,
    load_sem,
    x_send,
    x_recv,
    p_send,
    p_recv,
    r_send,
    r_recv,
    t_send,
    t_recv,
    q_send,
    q_recv,
    m_send,
    m_recv,
):
    rows, width = feat_ref.shape
    k_shard = kf.shape[1]
    half = k_shard // 2
    z_size = bricks // 2
    piece = half // z_size
    lanes = width // PARTS
    a = lax.axis_index("atom")
    g = lax.axis_index("kvec")
    z = lax.div(a, 2)
    c = lax.rem(a, 2)
    partner = 2 * z + 1 - c
    count = count_ref[a]

    def z_peer(d):
        return 2 * lax.rem(z + d, z_size) + c

    def z_from(d):
        return lax.rem(z + z_size - d, z_size)

    barrier = pltpu.get_barrier_semaphore()
    for d in range(1, groups):
        pl.semaphore_signal(
            barrier, inc=1, device_id={"kvec": lax.rem(g + d, groups)}, device_id_type=MESH
        )
    for d in range(1, z_size):
        pl.semaphore_signal(
            barrier, inc=1, device_id={"atom": z_peer(d)}, device_id_type=MESH
        )
    pl.semaphore_signal(barrier, inc=1, device_id={"atom": partner}, device_id_type=MESH)

    loads = []
    for i, (src, dst) in enumerate(
        ((kf_hbm, kf), (vw_hbm, vw), (mix_hbm, mix), (ow_hbm, ow), (up_hbm, up), (down_hbm, down))
    ):
        loads.append(pltpu.make_async_copy(src, dst, load_sem.at[i]))
        loads[-1].start()

    pl.semaphore_wait(barrier, groups - 1 + z_size)

    def x_copy(h, d):
        return pltpu.make_async_remote_copy(
            src_ref=feat_ref.at[:, h * lanes : (h + 1) * lanes],
            dst_ref=xbuf.at[h, g],
            send_sem=x_send.at[h, d - 1],
            recv_sem=x_recv.at[h, d - 1],
            device_id={"kvec": lax.rem(g + d, groups)},
            device_id_type=MESH,
        )

    for h in range(PARTS):
        for d in range(1, groups):
            x_copy(h, d).start()

    def table(dst, j, phase, lead, step):
        def one(i, carry):
            at = pl.multiple_of(i * step, step)
            x = phase[pl.ds(at, step), :]
            r = x - jnp.floor(x + 0.5)
            y = r * r
            s = r * horner(SIN_POLY, y)
            co = horner(COS_POLY, y)
            s2 = s + s
            chi, clo = split(1.0 - s2 * s)
            shi, slo = split(s2 * co)
            dst[0, j, pl.ds(at, step), :] = chi
            dst[1, j, pl.ds(at, step), :] = clo
            dst[2, j, pl.ds(at, step), :] = shi
            dst[3, j, pl.ds(at, step), :] = slo
            return carry

        lax.fori_loop(0, lead // step, one, 0, unroll=2)

    parts = frac_ref[...]
    stacked = jnp.concatenate(
        [
            (parts >> 5).astype(f32) * (1.0 / 32),
            (parts & 31).astype(f32) * (1.0 / 1024),
            jnp.zeros((2, groups * rows), f32),
        ],
        axis=0,
    )
    for j in range(groups):
        frac[j] = stacked[:, j * rows : (j + 1) * rows].astype(bf16)
    wave = wave_ref[...].astype(f32)
    wave = jnp.concatenate([wave, wave, jnp.zeros((2, k_shard), f32)], axis=0).astype(bf16)
    first = (((0,), (0,)), ((), ()))

    def make_tables(j, carry):
        phase_t[...] = lax.dot_general(wave, frac[j], first, preferred_element_type=f32)
        table(ct, j, phase_t, k_shard, 32)
        return carry

    def more_tables(j, carry):
        phase_n[...] = lax.dot_general(frac[j], wave, first, preferred_element_type=f32)
        table(cn, j, phase_n, rows, 16)
        return carry

    lax.fori_loop(0, groups, make_tables, 0)

    def live(j, cols):
        spot = lax.broadcasted_iota(jnp.int32, (rows, cols), 0) + j * rows
        return spot < count

    def twice(hi, lo, pair):
        both = mm(hi, pair)
        return both[:, :lanes] + (both[:, lanes:] + mm(lo, pair[:, :lanes]))

    def gather_term(x, j):
        v = jnp.concatenate(split(jnp.where(live(j, lanes), x, 0.0)), axis=1)
        re = twice(ct[0, j], ct[1, j], v)
        im = twice(ct[2, j], ct[3, j], v)
        return (
            re.reshape(2, z_size, piece, lanes),
            im.reshape(2, z_size, piece, lanes),
        )

    def own_block(h):
        re, im = gather_term(feat_ref[:, h * lanes : (h + 1) * lanes], g)
        sacc[h, :, :, 0] = re
        sacc[h, :, :, 1] = im

    def other_blocks(h):
        def take_block(d, carry):
            j = lax.rem(g + groups - d, groups)
            x_copy(h, d).wait_recv()
            re, im = gather_term(xbuf[h, j], j)
            sacc[h, :, :, 0] += re
            sacc[h, :, :, 1] += im
            return carry

        lax.fori_loop(1, groups, take_block, 0)

    def pair(h):
        return pltpu.make_async_remote_copy(
            src_ref=sacc.at[h, 1 - c],
            dst_ref=pbuf.at[h],
            send_sem=p_send.at[h],
            recv_sem=p_recv.at[h],
            device_id={"atom": partner},
            device_id_type=MESH,
        )

    def r_copy(h, d):
        return pltpu.make_async_remote_copy(
            src_ref=ssum.at[h, lax.rem(z + d, z_size)],
            dst_ref=rbuf.at[h, d - 1],
            send_sem=r_send.at[h, d - 1],
            recv_sem=r_recv.at[h, d - 1],
            device_id={"atom": z_peer(d)},
            device_id_type=MESH,
        )

    own_block(0)
    for h in range(PARTS):
        other_blocks(h)
        pair(h).start()
        if h + 1 < PARTS:
            own_block(h + 1)
        pair(h).wait_recv()
        ssum[h] = sacc[h, c] + pbuf[h]
        for d in range(1, z_size):
            r_copy(h, d).start()

    lax.fori_loop(0, groups, more_tables, 0)
    for load in loads:
        load.wait()
    vws = split(vw[...])
    mix_re = split(mix[0])
    mix_im = split(mix[1])
    totals = []
    for h in range(PARTS):
        total = ssum[h, z]
        for d in range(1, z_size):
            r_copy(h, d).wait_recv()
            total = total + rbuf[h, d - 1]
        totals.append(total.reshape(2 * piece, lanes))
    sv = mm3(split(jnp.concatenate(totals, axis=1)), vws)
    sre = sv[:piece]
    sim = -sv[piece:]
    at = pl.multiple_of(c * half + z * piece, piece)
    k_re = kf[0, pl.ds(at, piece), :]
    k_im = kf[1, pl.ds(at, piece), :]
    u_re = split(sre * k_re - sim * k_im)
    u_im = split(sre * k_im + sim * k_re)

    def t_copy(h, d):
        return pltpu.make_async_remote_copy(
            src_ref=tsl.at[h],
            dst_ref=tbuf.at[h, c, z],
            send_sem=t_send.at[h, d - 1],
            recv_sem=t_recv.at[h, d - 1],
            device_id={"atom": z_peer(d)},
            device_id_type=MESH,
        )

    def q_copy(h, d):
        return pltpu.make_async_remote_copy(
            src_ref=tsl.at[h] if d == 0 else tbuf.at[h, c, z_from(d)],
            dst_ref=tbuf.at[h, c, z_from(d)],
            send_sem=q_send.at[h, d],
            recv_sem=q_recv.at[h, d],
            device_id={"atom": partner},
            device_id_type=MESH,
        )

    def m_copy(h, d):
        return pltpu.make_async_remote_copy(
            src_ref=mbuf.at[h, d - 1],
            dst_ref=gbuf.at[h, d - 1],
            send_sem=m_send.at[h, d - 1],
            recv_sem=m_recv.at[h, d - 1],
            device_id={"kvec": lax.rem(g + d, groups)},
            device_id_type=MESH,
        )

    out_re = (mm3(u_re, mix_re) - mm3(u_im, mix_im)) * normalizer
    out_im = (mm3(u_re, mix_im) + mm3(u_im, mix_re)) * normalizer
    for h in range(PARTS):
        tsl[h, 0] = out_re[:, h * lanes : (h + 1) * lanes]
        tsl[h, 1] = out_im[:, h * lanes : (h + 1) * lanes]
        for d in range(1, z_size):
            t_copy(h, d).start()
        q_copy(h, 0).start()
        tbuf[h, c, z] = tsl[h]

    owns = []
    for h in range(PARTS):
        for d in range(1, z_size):
            t_copy(h, d).wait_recv()
            q_copy(h, d).start()
        for d in range(z_size):
            q_copy(h, d).wait_recv()
        t_re = jnp.concatenate(split(tbuf[h, :, :, 0].reshape(k_shard, lanes)), axis=1)
        t_im = jnp.concatenate(split(tbuf[h, :, :, 1].reshape(k_shard, lanes)), axis=1)

        def message(j):
            return twice(cn[0, j], cn[1, j], t_re) - twice(cn[2, j], cn[3, j], t_im)

        def give_block(d, carry):
            mbuf[h, d - 1] = message(lax.rem(g + d, groups))
            m_copy(h, d).start()
            return carry

        lax.fori_loop(1, groups, give_block, 0)
        owns.append(message(g))
    for h in range(PARTS):
        for d in range(1, groups):
            m_copy(h, d).wait_recv()
            owns[h] = owns[h] + gbuf[h, d - 1]
    own = jnp.concatenate(owns, axis=1)

    residual = feat_ref[...] + mm3(split(own), split(ow[...]))
    scale = lax.rsqrt(jnp.mean(residual * residual, axis=1, keepdims=True) + 1e-06)
    normed = residual * scale * gain_ref[...]
    raised = mm3(split(normed), split(up[...]))
    hidden = raised / (1.0 + jnp.exp(-raised))
    result = residual + mm3(split(hidden), split(down[...]))
    out_ref[...] = jnp.where(live(g, width), result, 0.0)

    for h in range(PARTS):
        pair(h).wait_send()
        for d in range(1, groups):
            x_copy(h, d).wait_send()
            m_copy(h, d).wait_send()
        for d in range(1, z_size):
            r_copy(h, d).wait_send()
            t_copy(h, d).wait_send()
        for d in range(z_size):
            q_copy(h, d).wait_send()


def shards(
    features,
    fractions,
    wave_index,
    brick_count,
    value_weight,
    k_filter,
    mix_weight,
    out_weight,
    norm_gain,
    up_weight,
    down_weight,
):
    rows, width = features.shape
    groups = lax.axis_size("kvec")
    bricks = lax.axis_size("atom")
    k_shard = wave_index.shape[1]
    hidden = up_weight.shape[1]
    capacity = rows * groups
    z_size = bricks // 2
    piece = k_shard // bricks
    lanes = width // PARTS
    normalizer = 1.0 / math.sqrt(bricks * capacity // 2 * (k_shard * groups))
    vmem = pl.BlockSpec(memory_space=pltpu.VMEM)
    hbm = pl.BlockSpec(memory_space=pl.ANY)
    dma = pltpu.SemaphoreType.DMA
    return pl.pallas_call(
        functools.partial(kernel, groups, bricks, normalizer),
        out_shape=jax.ShapeDtypeStruct((rows, width), f32),
        in_specs=[pl.BlockSpec(memory_space=pltpu.SMEM)] + [vmem] * 4 + [hbm] * 6,
        out_specs=vmem,
        scratch_shapes=[
            pltpu.VMEM((2, k_shard, width), f32),
            pltpu.VMEM((width, width), f32),
            pltpu.VMEM((2, width, width), f32),
            pltpu.VMEM((width, width), f32),
            pltpu.VMEM((width, hidden), f32),
            pltpu.VMEM((hidden, width), f32),
            pltpu.VMEM((groups, 8, rows), bf16),
            pltpu.VMEM((k_shard, rows), f32),
            pltpu.VMEM((rows, k_shard), f32),
            pltpu.VMEM((4, groups, k_shard, rows), bf16),
            pltpu.VMEM((4, groups, rows, k_shard), bf16),
            pltpu.VMEM((PARTS, groups, rows, lanes), f32),
            pltpu.VMEM((PARTS, 2, z_size, 2, piece, lanes), f32),
            pltpu.VMEM((PARTS, z_size, 2, piece, lanes), f32),
            pltpu.VMEM((PARTS, z_size, 2, piece, lanes), f32),
            pltpu.VMEM((PARTS, z_size - 1, 2, piece, lanes), f32),
            pltpu.VMEM((PARTS, 2, piece, lanes), f32),
            pltpu.VMEM((PARTS, 2, z_size, 2, piece, lanes), f32),
            pltpu.VMEM((PARTS, groups - 1, rows, lanes), f32),
            pltpu.VMEM((PARTS, groups - 1, rows, lanes), f32),
            dma((6,)),
            dma((PARTS, groups - 1)),
            dma((PARTS, groups - 1)),
            dma((PARTS,)),
            dma((PARTS,)),
            dma((PARTS, z_size - 1)),
            dma((PARTS, z_size - 1)),
            dma((PARTS, z_size - 1)),
            dma((PARTS, z_size - 1)),
            dma((PARTS, z_size)),
            dma((PARTS, z_size)),
            dma((PARTS, groups - 1)),
            dma((PARTS, groups - 1)),
        ],
        compiler_params=pltpu.CompilerParams(
            collective_id=0, has_side_effects=True, vmem_limit_bytes=56 * 1024 * 1024
        ),
    )(
        brick_count,
        features,
        fractions,
        wave_index,
        norm_gain.reshape(1, width),
        k_filter,
        value_weight,
        mix_weight,
        out_weight,
        up_weight,
        down_weight,
    )


def solution(mesh):
    return jax.shard_map(
        shards,
        mesh=mesh,
        in_specs=(
            P(("atom", "kvec"), None),
            P(None, "atom"),
            P(None, "kvec"),
            P(),
            P(),
            P(None, "kvec", None),
            P(),
            P(),
            P(),
            P(),
            P(),
        ),
        out_specs=P(("atom", "kvec"), None),
        check_vma=False,
    )
```

```python
import functools
import math

import jax
import jax.numpy as jnp
from jax import lax
from jax.experimental import pallas as pl
from jax.experimental.pallas import tpu as pltpu
from jax.sharding import PartitionSpec as P

SIN_POLY = (3.141592640130707, -5.167710083507862, 2.550077523214134, -0.5982912856178576, 0.0776576603009221)
COS_POLY = (0.9999999997799045, -4.9348021370788056, 4.058709159555753, -1.3352120030448535, 0.23493731379172217, -0.024396324310603436)
PARTS = 2
MESH = pl.DeviceIdType.MESH
f32 = jnp.float32
bf16 = jnp.bfloat16


def horner(coefs, y):
    acc = jnp.full_like(y, coefs[-1])
    for c in coefs[-2::-1]:
        acc = acc * y + c
    return acc


def split(x):
    hi = x.astype(bf16)
    return hi, (x - hi.astype(f32)).astype(bf16)


def mm(a, b):
    return jnp.dot(a, b, preferred_element_type=f32)


def mm3(a, b):
    return mm(a[0], b[0]) + (mm(a[0], b[1]) + mm(a[1], b[0]))


def kernel(
    groups,
    bricks,
    normalizer,
    count_ref,
    feat_ref,
    frac_ref,
    wave_ref,
    gain_ref,
    kf_hbm,
    vw_hbm,
    mix_hbm,
    ow_hbm,
    up_hbm,
    down_hbm,
    out_ref,
    kf,
    vw,
    mix,
    ow,
    up,
    down,
    frac,
    phase_t,
    phase_n,
    ct,
    cn,
    xbuf,
    sacc,
    pbuf,
    ssum,
    rbuf,
    tsl,
    tbuf,
    mbuf,
    gbuf,
    load_sem,
    x_send,
    x_recv,
    p_send,
    p_recv,
    r_send,
    r_recv,
    t_send,
    t_recv,
    q_send,
    q_recv,
    m_send,
    m_recv,
):
    rows, width = feat_ref.shape
    k_shard = kf.shape[1]
    half = k_shard // 2
    z_size = bricks // 2
    piece = half // z_size
    lanes = width // PARTS
    a = lax.axis_index("atom")
    g = lax.axis_index("kvec")
    z = lax.div(a, 2)
    c = lax.rem(a, 2)
    partner = 2 * z + 1 - c
    count = count_ref[a]

    def z_peer(d):
        return 2 * lax.rem(z + d, z_size) + c

    def z_from(d):
        return lax.rem(z + z_size - d, z_size)

    barrier = pltpu.get_barrier_semaphore()
    for d in range(1, groups):
        pl.semaphore_signal(
            barrier, inc=1, device_id={"kvec": lax.rem(g + d, groups)}, device_id_type=MESH
        )
    for d in range(1, z_size):
        pl.semaphore_signal(
            barrier, inc=1, device_id={"atom": z_peer(d)}, device_id_type=MESH
        )
    pl.semaphore_signal(barrier, inc=1, device_id={"atom": partner}, device_id_type=MESH)

    loads = []
    for i, (src, dst) in enumerate(
        ((kf_hbm, kf), (vw_hbm, vw), (mix_hbm, mix), (ow_hbm, ow), (up_hbm, up), (down_hbm, down))
    ):
        loads.append(pltpu.make_async_copy(src, dst, load_sem.at[i]))
        loads[-1].start()

    pl.semaphore_wait(barrier, groups - 1 + z_size)

    def x_copy(h, d):
        return pltpu.make_async_remote_copy(
            src_ref=feat_ref.at[:, h * lanes : (h + 1) * lanes],
            dst_ref=xbuf.at[h, g],
            send_sem=x_send.at[h, d - 1],
            recv_sem=x_recv.at[h, d - 1],
            device_id={"kvec": lax.rem(g + d, groups)},
            device_id_type=MESH,
        )

    square = groups == 4
    top, low = pl.ds(0, rows // 2), pl.ds(rows // 2, rows // 2)
    side = g + 1 - 2 * lax.rem(g, 2)
    over = lax.rem(g + 2, 4)
    cross = lax.rem(side + 2, 4)

    def x_hop(h, i):
        if i < 2:
            src, slot = feat_ref.at[:, h * lanes : (h + 1) * lanes], xbuf.at[h, g]
        elif i == 2:
            src = slot = xbuf.at[h, over, top]
        else:
            src = slot = xbuf.at[h, side, low]
        return pltpu.make_async_remote_copy(
            src_ref=src,
            dst_ref=slot,
            send_sem=x_send.at[h, i],
            recv_sem=x_recv.at[h, i],
            device_id={"kvec": over if i % 2 else side},
            device_id_type=MESH,
        )

    for h in range(PARTS):
        if square:
            x_hop(h, 0).start()
            x_hop(h, 1).start()
            continue
        for d in range(1, groups):
            x_copy(h, d).start()

    def table(dst, j, phase, lead, step):
        def one(i, carry):
            at = pl.multiple_of(i * step, step)
            x = phase[pl.ds(at, step), :]
            r = x - jnp.floor(x + 0.5)
            y = r * r
            s = r * horner(SIN_POLY, y)
            co = horner(COS_POLY, y)
            s2 = s + s
            chi, clo = split(1.0 - s2 * s)
            shi, slo = split(s2 * co)
            dst[0, j, pl.ds(at, step), :] = chi
            dst[1, j, pl.ds(at, step), :] = clo
            dst[2, j, pl.ds(at, step), :] = shi
            dst[3, j, pl.ds(at, step), :] = slo
            return carry

        lax.fori_loop(0, lead // step, one, 0, unroll=2)

    parts = frac_ref[...]
    stacked = jnp.concatenate(
        [
            (parts >> 5).astype(f32) * (1.0 / 32),
            (parts & 31).astype(f32) * (1.0 / 1024),
            jnp.zeros((2, groups * rows), f32),
        ],
        axis=0,
    )
    for j in range(groups):
        frac[j] = stacked[:, j * rows : (j + 1) * rows].astype(bf16)
    wave = wave_ref[...].astype(f32)
    wave = jnp.concatenate([wave, wave, jnp.zeros((2, k_shard), f32)], axis=0).astype(bf16)
    first = (((0,), (0,)), ((), ()))

    def make_tables(j, carry):
        phase_t[...] = lax.dot_general(wave, frac[j], first, preferred_element_type=f32)
        table(ct, j, phase_t, k_shard, 32)
        return carry

    def more_tables(j, carry):
        phase_n[...] = lax.dot_general(frac[j], wave, first, preferred_element_type=f32)
        table(cn, j, phase_n, rows, 16)
        return carry

    lax.fori_loop(0, groups, make_tables, 0)

    def live(j, cols):
        spot = lax.broadcasted_iota(jnp.int32, (rows, cols), 0) + j * rows
        return spot < count

    def twice(hi, lo, pair):
        both = mm(hi, pair)
        return both[:, :lanes] + (both[:, lanes:] + mm(lo, pair[:, :lanes]))

    def gather_term(x, j):
        v = jnp.concatenate(split(jnp.where(live(j, lanes), x, 0.0)), axis=1)
        re = twice(ct[0, j], ct[1, j], v)
        im = twice(ct[2, j], ct[3, j], v)
        return (
            re.reshape(2, z_size, piece, lanes),
            im.reshape(2, z_size, piece, lanes),
        )

    def own_block(h):
        re, im = gather_term(feat_ref[:, h * lanes : (h + 1) * lanes], g)
        sacc[h, :, :, 0] = re
        sacc[h, :, :, 1] = im

    def add_block(h, j):
        re, im = gather_term(xbuf[h, j], j)
        sacc[h, :, :, 0] += re
        sacc[h, :, :, 1] += im

    def square_blocks(h):
        x_hop(h, 0).wait_recv()
        x_hop(h, 3).start()
        x_hop(h, 1).wait_recv()
        x_hop(h, 2).start()
        add_block(h, side)
        add_block(h, over)
        x_hop(h, 2).wait_recv()
        x_hop(h, 3).wait_recv()
        add_block(h, cross)

    def other_blocks(h):
        def take_block(d, carry):
            j = lax.rem(g + groups - d, groups)
            x_copy(h, d).wait_recv()
            add_block(h, j)
            return carry

        lax.fori_loop(1, groups, take_block, 0)

    def pair(h):
        return pltpu.make_async_remote_copy(
            src_ref=sacc.at[h, 1 - c],
            dst_ref=pbuf.at[h],
            send_sem=p_send.at[h],
            recv_sem=p_recv.at[h],
            device_id={"atom": partner},
            device_id_type=MESH,
        )

    def r_copy(h, d):
        return pltpu.make_async_remote_copy(
            src_ref=ssum.at[h, lax.rem(z + d, z_size)],
            dst_ref=rbuf.at[h, d - 1],
            send_sem=r_send.at[h, d - 1],
            recv_sem=r_recv.at[h, d - 1],
            device_id={"atom": z_peer(d)},
            device_id_type=MESH,
        )

    own_block(0)
    for h in range(PARTS):
        (square_blocks if square else other_blocks)(h)
        pair(h).start()
        if h + 1 < PARTS:
            own_block(h + 1)
        pair(h).wait_recv()
        ssum[h] = sacc[h, c] + pbuf[h]
        for d in range(1, z_size):
            r_copy(h, d).start()

    lax.fori_loop(0, groups, more_tables, 0)
    for load in loads:
        load.wait()
    vws = split(vw[...])
    mix_re = split(mix[0])
    mix_im = split(mix[1])
    totals = []
    for h in range(PARTS):
        total = ssum[h, z]
        for d in range(1, z_size):
            r_copy(h, d).wait_recv()
            total = total + rbuf[h, d - 1]
        totals.append(total.reshape(2 * piece, lanes))
    sv = mm3(split(jnp.concatenate(totals, axis=1)), vws)
    sre = sv[:piece]
    sim = -sv[piece:]
    at = pl.multiple_of(c * half + z * piece, piece)
    k_re = kf[0, pl.ds(at, piece), :]
    k_im = kf[1, pl.ds(at, piece), :]
    u_re = split(sre * k_re - sim * k_im)
    u_im = split(sre * k_im + sim * k_re)

    def t_copy(h, d):
        return pltpu.make_async_remote_copy(
            src_ref=tsl.at[h],
            dst_ref=tbuf.at[h, c, z],
            send_sem=t_send.at[h, d - 1],
            recv_sem=t_recv.at[h, d - 1],
            device_id={"atom": z_peer(d)},
            device_id_type=MESH,
        )

    def q_copy(h, d):
        return pltpu.make_async_remote_copy(
            src_ref=tsl.at[h] if d == 0 else tbuf.at[h, c, z_from(d)],
            dst_ref=tbuf.at[h, c, z_from(d)],
            send_sem=q_send.at[h, d],
            recv_sem=q_recv.at[h, d],
            device_id={"atom": partner},
            device_id_type=MESH,
        )

    def m_copy(h, d):
        return pltpu.make_async_remote_copy(
            src_ref=mbuf.at[h, d - 1],
            dst_ref=gbuf.at[h, d - 1],
            send_sem=m_send.at[h, d - 1],
            recv_sem=m_recv.at[h, d - 1],
            device_id={"kvec": lax.rem(g + d, groups)},
            device_id_type=MESH,
        )

    def m_hop(h, i):
        half_rows = low if i % 2 else top
        if i < 2:
            src, slot = mbuf.at[h, 2, half_rows], gbuf.at[h, 0, half_rows]
        else:
            src, slot = mbuf.at[h, i - 2], gbuf.at[h, i - 1]
        return pltpu.make_async_remote_copy(
            src_ref=src,
            dst_ref=slot,
            send_sem=m_send.at[h, i],
            recv_sem=m_recv.at[h, i],
            device_id={"kvec": over if i % 2 else side},
            device_id_type=MESH,
        )

    out_re = (mm3(u_re, mix_re) - mm3(u_im, mix_im)) * normalizer
    out_im = (mm3(u_re, mix_im) + mm3(u_im, mix_re)) * normalizer
    for h in range(PARTS):
        tsl[h, 0] = out_re[:, h * lanes : (h + 1) * lanes]
        tsl[h, 1] = out_im[:, h * lanes : (h + 1) * lanes]
        for d in range(1, z_size):
            t_copy(h, d).start()
        q_copy(h, 0).start()
        tbuf[h, c, z] = tsl[h]

    owns = []
    for h in range(PARTS):
        for d in range(1, z_size):
            t_copy(h, d).wait_recv()
            q_copy(h, d).start()
        for d in range(z_size):
            q_copy(h, d).wait_recv()
        t_re = jnp.concatenate(split(tbuf[h, :, :, 0].reshape(k_shard, lanes)), axis=1)
        t_im = jnp.concatenate(split(tbuf[h, :, :, 1].reshape(k_shard, lanes)), axis=1)

        def message(j):
            return twice(cn[0, j], cn[1, j], t_re) - twice(cn[2, j], cn[3, j], t_im)

        def give_block(d, carry):
            mbuf[h, d - 1] = message(lax.rem(g + d, groups))
            m_copy(h, d).start()
            return carry

        if square:
            mbuf[h, 2] = message(cross)
            m_hop(h, 0).start()
            m_hop(h, 1).start()
            mbuf[h, 0] = message(side)
            mbuf[h, 1] = message(over)
            m_hop(h, 1).wait_recv()
            mbuf[h, 0, low] += gbuf[h, 0, low]
            m_hop(h, 2).start()
            m_hop(h, 0).wait_recv()
            mbuf[h, 1, top] += gbuf[h, 0, top]
            m_hop(h, 3).start()
        else:
            lax.fori_loop(1, groups, give_block, 0)
        owns.append(message(g))
    for h in range(PARTS):
        if square:
            m_hop(h, 2).wait_recv()
            m_hop(h, 3).wait_recv()
            owns[h] = owns[h] + gbuf[h, 1] + gbuf[h, 2]
            continue
        for d in range(1, groups):
            m_copy(h, d).wait_recv()
            owns[h] = owns[h] + gbuf[h, d - 1]
    own = jnp.concatenate(owns, axis=1)

    residual = feat_ref[...] + mm3(split(own), split(ow[...]))
    scale = lax.rsqrt(jnp.mean(residual * residual, axis=1, keepdims=True) + 1e-06)
    normed = residual * scale * gain_ref[...]
    raised = mm3(split(normed), split(up[...]))
    hidden = raised / (1.0 + jnp.exp(-raised))
    result = residual + mm3(split(hidden), split(down[...]))
    out_ref[...] = jnp.where(live(g, width), result, 0.0)

    for h in range(PARTS):
        pair(h).wait_send()
        for d in range(1, groups):
            if not square:
                x_copy(h, d).wait_send()
                m_copy(h, d).wait_send()
        for i in range(4 if square else 0):
            x_hop(h, i).wait_send()
            m_hop(h, i).wait_send()
        for d in range(1, z_size):
            r_copy(h, d).wait_send()
            t_copy(h, d).wait_send()
        for d in range(z_size):
            q_copy(h, d).wait_send()


def shards(
    features,
    fractions,
    wave_index,
    brick_count,
    value_weight,
    k_filter,
    mix_weight,
    out_weight,
    norm_gain,
    up_weight,
    down_weight,
):
    rows, width = features.shape
    groups = lax.axis_size("kvec")
    bricks = lax.axis_size("atom")
    k_shard = wave_index.shape[1]
    hidden = up_weight.shape[1]
    capacity = rows * groups
    z_size = bricks // 2
    piece = k_shard // bricks
    lanes = width // PARTS
    normalizer = 1.0 / math.sqrt(bricks * capacity // 2 * (k_shard * groups))
    vmem = pl.BlockSpec(memory_space=pltpu.VMEM)
    hbm = pl.BlockSpec(memory_space=pl.ANY)
    dma = pltpu.SemaphoreType.DMA
    return pl.pallas_call(
        functools.partial(kernel, groups, bricks, normalizer),
        out_shape=jax.ShapeDtypeStruct((rows, width), f32),
        in_specs=[pl.BlockSpec(memory_space=pltpu.SMEM)] + [vmem] * 4 + [hbm] * 6,
        out_specs=vmem,
        scratch_shapes=[
            pltpu.VMEM((2, k_shard, width), f32),
            pltpu.VMEM((width, width), f32),
            pltpu.VMEM((2, width, width), f32),
            pltpu.VMEM((width, width), f32),
            pltpu.VMEM((width, hidden), f32),
            pltpu.VMEM((hidden, width), f32),
            pltpu.VMEM((groups, 8, rows), bf16),
            pltpu.VMEM((k_shard, rows), f32),
            pltpu.VMEM((rows, k_shard), f32),
            pltpu.VMEM((4, groups, k_shard, rows), bf16),
            pltpu.VMEM((4, groups, rows, k_shard), bf16),
            pltpu.VMEM((PARTS, groups, rows, lanes), f32),
            pltpu.VMEM((PARTS, 2, z_size, 2, piece, lanes), f32),
            pltpu.VMEM((PARTS, z_size, 2, piece, lanes), f32),
            pltpu.VMEM((PARTS, z_size, 2, piece, lanes), f32),
            pltpu.VMEM((PARTS, z_size - 1, 2, piece, lanes), f32),
            pltpu.VMEM((PARTS, 2, piece, lanes), f32),
            pltpu.VMEM((PARTS, 2, z_size, 2, piece, lanes), f32),
            pltpu.VMEM((PARTS, groups - 1, rows, lanes), f32),
            pltpu.VMEM((PARTS, groups - 1, rows, lanes), f32),
            dma((6,)),
            dma((PARTS, max(groups - 1, 4))),
            dma((PARTS, max(groups - 1, 4))),
            dma((PARTS,)),
            dma((PARTS,)),
            dma((PARTS, z_size - 1)),
            dma((PARTS, z_size - 1)),
            dma((PARTS, z_size - 1)),
            dma((PARTS, z_size - 1)),
            dma((PARTS, z_size)),
            dma((PARTS, z_size)),
            dma((PARTS, max(groups - 1, 4))),
            dma((PARTS, max(groups - 1, 4))),
        ],
        compiler_params=pltpu.CompilerParams(
            collective_id=0, has_side_effects=True, vmem_limit_bytes=56 * 1024 * 1024
        ),
    )(
        brick_count,
        features,
        fractions,
        wave_index,
        norm_gain.reshape(1, width),
        k_filter,
        value_weight,
        mix_weight,
        out_weight,
        up_weight,
        down_weight,
    )


def solution(mesh):
    return jax.shard_map(
        shards,
        mesh=mesh,
        in_specs=(
            P(("atom", "kvec"), None),
            P(None, "atom"),
            P(None, "kvec"),
            P(),
            P(),
            P(None, "kvec", None),
            P(),
            P(),
            P(),
            P(),
            P(),
        ),
        out_specs=P(("atom", "kvec"), None),
        check_vma=False,
    )
```

```python
import functools
import math

import jax
import jax.numpy as jnp
from jax import lax
from jax.experimental import pallas as pl
from jax.experimental.pallas import tpu as pltpu
from jax.sharding import PartitionSpec as P

SIN_POLY = (3.141592640130707, -5.167710083507862, 2.550077523214134, -0.5982912856178576, 0.0776576603009221)
COS_POLY = (0.9999999997799045, -4.9348021370788056, 4.058709159555753, -1.3352120030448535, 0.23493731379172217, -0.024396324310603436)
PARTS = 2
MESH = pl.DeviceIdType.MESH
f32 = jnp.float32
bf16 = jnp.bfloat16


def horner(coefs, y):
    acc = jnp.full_like(y, coefs[-1])
    for c in coefs[-2::-1]:
        acc = acc * y + c
    return acc


def split(x):
    hi = x.astype(bf16)
    return hi, (x - hi.astype(f32)).astype(bf16)


def mm(a, b):
    return jnp.dot(a, b, preferred_element_type=f32)


def mm3(a, b):
    return mm(a[0], b[0]) + (mm(a[0], b[1]) + mm(a[1], b[0]))


def kernel(
    groups,
    bricks,
    normalizer,
    count_ref,
    feat_ref,
    frac_ref,
    wave_ref,
    gain_ref,
    kf_hbm,
    vw_hbm,
    mix_hbm,
    ow_hbm,
    up_hbm,
    down_hbm,
    out_ref,
    kf,
    vw,
    mix,
    ow,
    up,
    down,
    frac,
    phase_t,
    phase_n,
    ct,
    cn,
    xbuf,
    sacc,
    pbuf,
    ssum,
    rbuf,
    tsl,
    tbuf,
    mbuf,
    gbuf,
    load_sem,
    x_send,
    x_recv,
    p_send,
    p_recv,
    r_send,
    r_recv,
    t_send,
    t_recv,
    q_send,
    q_recv,
    m_send,
    m_recv,
):
    rows, width = feat_ref.shape
    k_shard = kf.shape[1]
    half = k_shard // 2
    z_size = bricks // 2
    piece = half // z_size
    lanes = width // PARTS
    a = lax.axis_index("atom")
    g = lax.axis_index("kvec")
    z = lax.div(a, 2)
    c = lax.rem(a, 2)
    partner = 2 * z + 1 - c
    count = count_ref[a]

    def z_peer(d):
        return 2 * lax.rem(z + d, z_size) + c

    def z_from(d):
        return lax.rem(z + z_size - d, z_size)

    barrier = pltpu.get_barrier_semaphore()
    for d in range(1, groups):
        pl.semaphore_signal(
            barrier, inc=1, device_id={"kvec": lax.rem(g + d, groups)}, device_id_type=MESH
        )
    for d in range(1, z_size):
        pl.semaphore_signal(
            barrier, inc=1, device_id={"atom": z_peer(d)}, device_id_type=MESH
        )
    pl.semaphore_signal(barrier, inc=1, device_id={"atom": partner}, device_id_type=MESH)

    loads = []
    for i, (src, dst) in enumerate(
        ((kf_hbm, kf), (vw_hbm, vw), (mix_hbm, mix), (ow_hbm, ow), (up_hbm, up), (down_hbm, down))
    ):
        loads.append(pltpu.make_async_copy(src, dst, load_sem.at[i]))
        loads[-1].start()

    pl.semaphore_wait(barrier, groups - 1 + z_size)

    def x_copy(h, d):
        return pltpu.make_async_remote_copy(
            src_ref=feat_ref.at[:, h * lanes : (h + 1) * lanes],
            dst_ref=xbuf.at[h, g],
            send_sem=x_send.at[h, d - 1],
            recv_sem=x_recv.at[h, d - 1],
            device_id={"kvec": lax.rem(g + d, groups)},
            device_id_type=MESH,
        )

    square = groups == 4
    top, low = pl.ds(0, rows // 2), pl.ds(rows // 2, rows // 2)
    side = g + 1 - 2 * lax.rem(g, 2)
    over = lax.rem(g + 2, 4)
    cross = lax.rem(side + 2, 4)

    def x_hop(h, i):
        if i < 2:
            src, slot = feat_ref.at[:, h * lanes : (h + 1) * lanes], xbuf.at[h, g]
        elif i == 2:
            src = slot = xbuf.at[h, over, top]
        else:
            src = slot = xbuf.at[h, side, low]
        return pltpu.make_async_remote_copy(
            src_ref=src,
            dst_ref=slot,
            send_sem=x_send.at[h, i],
            recv_sem=x_recv.at[h, i],
            device_id={"kvec": over if i % 2 else side},
            device_id_type=MESH,
        )

    for h in range(PARTS):
        if square:
            x_hop(h, 0).start()
            x_hop(h, 1).start()
            continue
        for d in range(1, groups):
            x_copy(h, d).start()

    def table(dst, j, phase, lead, step):
        def one(i, carry):
            at = pl.multiple_of(i * step, step)
            x = phase[pl.ds(at, step), :]
            r = x - jnp.floor(x + 0.5)
            y = r * r
            s = r * horner(SIN_POLY, y)
            co = horner(COS_POLY, y)
            s2 = s + s
            chi, clo = split(1.0 - s2 * s)
            shi, slo = split(s2 * co)
            dst[0, j, pl.ds(at, step), :] = chi
            dst[1, j, pl.ds(at, step), :] = clo
            dst[2, j, pl.ds(at, step), :] = shi
            dst[3, j, pl.ds(at, step), :] = slo
            return carry

        lax.fori_loop(0, lead // step, one, 0, unroll=2)

    parts = frac_ref[...]
    stacked = jnp.concatenate(
        [
            (parts >> 5).astype(f32) * (1.0 / 32),
            (parts & 31).astype(f32) * (1.0 / 1024),
            jnp.zeros((2, groups * rows), f32),
        ],
        axis=0,
    )
    for j in range(groups):
        frac[j] = stacked[:, j * rows : (j + 1) * rows].astype(bf16)
    wave = wave_ref[...].astype(f32)
    wave = jnp.concatenate([wave, wave, jnp.zeros((2, k_shard), f32)], axis=0).astype(bf16)
    first = (((0,), (0,)), ((), ()))

    def make_tables(j, carry):
        phase_t[...] = lax.dot_general(wave, frac[j], first, preferred_element_type=f32)
        table(ct, j, phase_t, k_shard, 32)
        return carry

    def more_tables(j, carry):
        phase_n[...] = lax.dot_general(frac[j], wave, first, preferred_element_type=f32)
        table(cn, j, phase_n, rows, 16)
        return carry

    lax.fori_loop(0, groups, make_tables, 0)

    def live(j, cols):
        spot = lax.broadcasted_iota(jnp.int32, (rows, cols), 0) + j * rows
        return spot < count

    def twice(hi, lo, pair):
        both = mm(hi, pair)
        return both[:, :lanes] + (both[:, lanes:] + mm(lo, pair[:, :lanes]))

    def gather_term(x, j):
        v = jnp.concatenate(split(jnp.where(live(j, lanes), x, 0.0)), axis=1)
        re = twice(ct[0, j], ct[1, j], v)
        im = twice(ct[2, j], ct[3, j], v)
        return (
            re.reshape(2, z_size, piece, lanes),
            im.reshape(2, z_size, piece, lanes),
        )

    def own_block(h):
        re, im = gather_term(feat_ref[:, h * lanes : (h + 1) * lanes], g)
        sacc[h, :, :, 0] = re
        sacc[h, :, :, 1] = im

    def add_block(h, j):
        re, im = gather_term(xbuf[h, j], j)
        sacc[h, :, :, 0] += re
        sacc[h, :, :, 1] += im

    def relay(h):
        x_hop(h, 0).wait_recv()
        x_hop(h, 3).start()
        x_hop(h, 1).wait_recv()
        x_hop(h, 2).start()

    def square_blocks(h):
        if h == 0:
            relay(0)
        add_block(h, side)
        add_block(h, over)
        if h + 1 < PARTS:
            relay(h + 1)
        x_hop(h, 2).wait_recv()
        x_hop(h, 3).wait_recv()
        add_block(h, cross)

    def other_blocks(h):
        def take_block(d, carry):
            j = lax.rem(g + groups - d, groups)
            x_copy(h, d).wait_recv()
            add_block(h, j)
            return carry

        lax.fori_loop(1, groups, take_block, 0)

    def pair(h):
        return pltpu.make_async_remote_copy(
            src_ref=sacc.at[h, 1 - c],
            dst_ref=pbuf.at[h],
            send_sem=p_send.at[h],
            recv_sem=p_recv.at[h],
            device_id={"atom": partner},
            device_id_type=MESH,
        )

    def r_copy(h, d):
        return pltpu.make_async_remote_copy(
            src_ref=ssum.at[h, lax.rem(z + d, z_size)],
            dst_ref=rbuf.at[h, d - 1],
            send_sem=r_send.at[h, d - 1],
            recv_sem=r_recv.at[h, d - 1],
            device_id={"atom": z_peer(d)},
            device_id_type=MESH,
        )

    own_block(0)
    for h in range(PARTS):
        (square_blocks if square else other_blocks)(h)
        pair(h).start()
        if h + 1 < PARTS:
            own_block(h + 1)
        pair(h).wait_recv()
        ssum[h] = sacc[h, c] + pbuf[h]
        for d in range(1, z_size):
            r_copy(h, d).start()

    lax.fori_loop(0, groups, more_tables, 0)
    for load in loads:
        load.wait()
    vws = split(vw[...])
    mix_re = split(mix[0])
    mix_im = split(mix[1])
    totals = []
    for h in range(PARTS):
        total = ssum[h, z]
        for d in range(1, z_size):
            r_copy(h, d).wait_recv()
            total = total + rbuf[h, d - 1]
        totals.append(total.reshape(2 * piece, lanes))
    sv = mm3(split(jnp.concatenate(totals, axis=1)), vws)
    sre = sv[:piece]
    sim = -sv[piece:]
    at = pl.multiple_of(c * half + z * piece, piece)
    k_re = kf[0, pl.ds(at, piece), :]
    k_im = kf[1, pl.ds(at, piece), :]
    u_all = split(
        jnp.concatenate([sre * k_re - sim * k_im, sre * k_im + sim * k_re], axis=0)
    )

    def t_copy(h, d):
        return pltpu.make_async_remote_copy(
            src_ref=tsl.at[h],
            dst_ref=tbuf.at[h, c, z],
            send_sem=t_send.at[h, d - 1],
            recv_sem=t_recv.at[h, d - 1],
            device_id={"atom": z_peer(d)},
            device_id_type=MESH,
        )

    def q_copy(h, d):
        return pltpu.make_async_remote_copy(
            src_ref=tsl.at[h] if d == 0 else tbuf.at[h, c, z_from(d)],
            dst_ref=tbuf.at[h, c, z_from(d)],
            send_sem=q_send.at[h, d],
            recv_sem=q_recv.at[h, d],
            device_id={"atom": partner},
            device_id_type=MESH,
        )

    def m_copy(h, d):
        return pltpu.make_async_remote_copy(
            src_ref=mbuf.at[h, d - 1],
            dst_ref=gbuf.at[h, d - 1],
            send_sem=m_send.at[h, d - 1],
            recv_sem=m_recv.at[h, d - 1],
            device_id={"kvec": lax.rem(g + d, groups)},
            device_id_type=MESH,
        )

    def m_hop(h, i):
        half_rows = low if i % 2 else top
        if i < 2:
            src, slot = mbuf.at[h, 2, half_rows], gbuf.at[h, 0, half_rows]
        else:
            src, slot = mbuf.at[h, i - 2], gbuf.at[h, i - 1]
        return pltpu.make_async_remote_copy(
            src_ref=src,
            dst_ref=slot,
            send_sem=m_send.at[h, i],
            recv_sem=m_recv.at[h, i],
            device_id={"kvec": over if i % 2 else side},
            device_id_type=MESH,
        )

    by_re = mm3(u_all, mix_re)
    by_im = mm3(u_all, mix_im)
    out_re = (by_re[:piece] - by_im[piece:]) * normalizer
    out_im = (by_im[:piece] + by_re[piece:]) * normalizer
    for h in range(PARTS):
        tsl[h, 0] = out_re[:, h * lanes : (h + 1) * lanes]
        tsl[h, 1] = out_im[:, h * lanes : (h + 1) * lanes]
        for d in range(1, z_size):
            t_copy(h, d).start()
        q_copy(h, 0).start()
        tbuf[h, c, z] = tsl[h]

    owns = []
    for h in range(PARTS):
        for d in range(1, z_size):
            t_copy(h, d).wait_recv()
            q_copy(h, d).start()
        for d in range(z_size):
            q_copy(h, d).wait_recv()
        t_re = jnp.concatenate(split(tbuf[h, :, :, 0].reshape(k_shard, lanes)), axis=1)
        t_im = jnp.concatenate(split(tbuf[h, :, :, 1].reshape(k_shard, lanes)), axis=1)

        def message(j):
            return twice(cn[0, j], cn[1, j], t_re) - twice(cn[2, j], cn[3, j], t_im)

        def give_block(d, carry):
            mbuf[h, d - 1] = message(lax.rem(g + d, groups))
            m_copy(h, d).start()
            return carry

        if square:
            mbuf[h, 2] = message(cross)
            m_hop(h, 0).start()
            m_hop(h, 1).start()
            mbuf[h, 0] = message(side)
            mbuf[h, 1] = message(over)
            m_hop(h, 1).wait_recv()
            mbuf[h, 0, low] += gbuf[h, 0, low]
            m_hop(h, 2).start()
            m_hop(h, 0).wait_recv()
            mbuf[h, 1, top] += gbuf[h, 0, top]
            m_hop(h, 3).start()
        else:
            lax.fori_loop(1, groups, give_block, 0)
        owns.append(message(g))
    for h in range(PARTS):
        if square:
            m_hop(h, 2).wait_recv()
            m_hop(h, 3).wait_recv()
            owns[h] = owns[h] + gbuf[h, 1] + gbuf[h, 2]
            continue
        for d in range(1, groups):
            m_copy(h, d).wait_recv()
            owns[h] = owns[h] + gbuf[h, d - 1]
    own = jnp.concatenate(owns, axis=1)

    residual = feat_ref[...] + mm3(split(own), split(ow[...]))
    scale = lax.rsqrt(jnp.mean(residual * residual, axis=1, keepdims=True) + 1e-06)
    normed = residual * scale * gain_ref[...]
    raised = mm3(split(normed), split(up[...]))
    hidden = raised / (1.0 + jnp.exp(-raised))
    result = residual + mm3(split(hidden), split(down[...]))
    out_ref[...] = jnp.where(live(g, width), result, 0.0)

    for h in range(PARTS):
        pair(h).wait_send()
        for d in range(1, groups):
            if not square:
                x_copy(h, d).wait_send()
                m_copy(h, d).wait_send()
        for i in range(4 if square else 0):
            x_hop(h, i).wait_send()
            m_hop(h, i).wait_send()
        for d in range(1, z_size):
            r_copy(h, d).wait_send()
            t_copy(h, d).wait_send()
        for d in range(z_size):
            q_copy(h, d).wait_send()


def shards(
    features,
    fractions,
    wave_index,
    brick_count,
    value_weight,
    k_filter,
    mix_weight,
    out_weight,
    norm_gain,
    up_weight,
    down_weight,
):
    rows, width = features.shape
    groups = lax.axis_size("kvec")
    bricks = lax.axis_size("atom")
    k_shard = wave_index.shape[1]
    hidden = up_weight.shape[1]
    capacity = rows * groups
    z_size = bricks // 2
    piece = k_shard // bricks
    lanes = width // PARTS
    normalizer = 1.0 / math.sqrt(bricks * capacity // 2 * (k_shard * groups))
    vmem = pl.BlockSpec(memory_space=pltpu.VMEM)
    hbm = pl.BlockSpec(memory_space=pl.ANY)
    dma = pltpu.SemaphoreType.DMA
    return pl.pallas_call(
        functools.partial(kernel, groups, bricks, normalizer),
        out_shape=jax.ShapeDtypeStruct((rows, width), f32),
        in_specs=[pl.BlockSpec(memory_space=pltpu.SMEM)] + [vmem] * 4 + [hbm] * 6,
        out_specs=vmem,
        scratch_shapes=[
            pltpu.VMEM((2, k_shard, width), f32),
            pltpu.VMEM((width, width), f32),
            pltpu.VMEM((2, width, width), f32),
            pltpu.VMEM((width, width), f32),
            pltpu.VMEM((width, hidden), f32),
            pltpu.VMEM((hidden, width), f32),
            pltpu.VMEM((groups, 8, rows), bf16),
            pltpu.VMEM((k_shard, rows), f32),
            pltpu.VMEM((rows, k_shard), f32),
            pltpu.VMEM((4, groups, k_shard, rows), bf16),
            pltpu.VMEM((4, groups, rows, k_shard), bf16),
            pltpu.VMEM((PARTS, groups, rows, lanes), f32),
            pltpu.VMEM((PARTS, 2, z_size, 2, piece, lanes), f32),
            pltpu.VMEM((PARTS, z_size, 2, piece, lanes), f32),
            pltpu.VMEM((PARTS, z_size, 2, piece, lanes), f32),
            pltpu.VMEM((PARTS, z_size - 1, 2, piece, lanes), f32),
            pltpu.VMEM((PARTS, 2, piece, lanes), f32),
            pltpu.VMEM((PARTS, 2, z_size, 2, piece, lanes), f32),
            pltpu.VMEM((PARTS, groups - 1, rows, lanes), f32),
            pltpu.VMEM((PARTS, groups - 1, rows, lanes), f32),
            dma((6,)),
            dma((PARTS, max(groups - 1, 4))),
            dma((PARTS, max(groups - 1, 4))),
            dma((PARTS,)),
            dma((PARTS,)),
            dma((PARTS, z_size - 1)),
            dma((PARTS, z_size - 1)),
            dma((PARTS, z_size - 1)),
            dma((PARTS, z_size - 1)),
            dma((PARTS, z_size)),
            dma((PARTS, z_size)),
            dma((PARTS, max(groups - 1, 4))),
            dma((PARTS, max(groups - 1, 4))),
        ],
        compiler_params=pltpu.CompilerParams(
            collective_id=0, has_side_effects=True, vmem_limit_bytes=56 * 1024 * 1024
        ),
    )(
        brick_count,
        features,
        fractions,
        wave_index,
        norm_gain.reshape(1, width),
        k_filter,
        value_weight,
        mix_weight,
        out_weight,
        up_weight,
        down_weight,
    )


def solution(mesh):
    return jax.shard_map(
        shards,
        mesh=mesh,
        in_specs=(
            P(("atom", "kvec"), None),
            P(None, "atom"),
            P(None, "kvec"),
            P(),
            P(),
            P(None, "kvec", None),
            P(),
            P(),
            P(),
            P(),
            P(),
        ),
        out_specs=P(("atom", "kvec"), None),
        check_vma=False,
    )
```
